32 devices in a mesh: band: 2 (over x), stn: 8 (over z, y), tile: 2 (over core).
Axes of the slice: x: 2, y: 2, z: 4, core: 2. Of those that a mesh axis runs over, the one named last changes fastest.
Arguments:
- raw_samples: float32 [2, 4096, 8240], P(None, ('band', 'stn', 'tile')), parts along dimension 1, may hold values from -6 to 6
- prototype: float32 [64], replicated, may hold values from -0.75 to 0.75
- beam_weight: bfloat16 [2, 512, 4096], P(None, None, ('band', 'stn', 'tile')), parts along dimension 2, may hold values from -0.09375 to 0.09375
Outputs:
- visibility: bfloat16 [64, 2, 2048, 2048], P(('band', 'stn'), None, None, 'tile'), parts along dimension 0
- beam_out: float32 [2, 64, 512, 256], P(None, ('band', 'stn'), 'tile'), parts along dimension 1
The draws below stay inside these ranges and needn't reach their ends.
There are 2 independent parts, one for each index of `band`. The reference program is written for one: setup_inputs(seed, part) draws one part's arguments, and reference() takes and returns one part's arrays. A program takes and returns all parts, laid end to end along the dimension named above; an argument that names none is the same for every part. Nothing has to cross between parts.
All inputs are finite; a program needn't handle non-finite values.
Results may differ from the reference program's by a relative error of at most 0.0055.
Values may be sent and summed in bfloat16 or wider, within the bound.
A program may use at most 192 MiB of HBM per device.

```python
import math
import jax
import jax.numpy as jnp
from jax import lax

INPUTS = 2048
FINE = 16
TAPS = 4
NBEAM = 512
DUMPS = 2
MD = 256
STN_BLOCKS = 8
CORE_BLOCKS = 2
SAMPLES = 8240


def block_levels(stream_key, shape, pieces, smallest, top_value):
    factor_of, own = 1.0, jax.random.fold_in(stream_key, 6)
    for dim, parts in pieces:
        steps = jnp.exp(jax.random.uniform(jax.random.fold_in(own, dim), (parts,), jnp.float32, smallest / len(pieces), top_value / len(pieces)))
        factor_of = factor_of * jnp.repeat(steps, shape[dim] // parts).reshape([-1 if axis == dim else 1 for axis in range(len(shape))])
    return factor_of


def bell_draw(stream_key, shape, spread, limit, pieces=(), held_as=jnp.bfloat16):
    result = jax.random.normal(stream_key, shape, jnp.float32) * spread
    if len(pieces) > 0:
        result = block_levels(stream_key, shape, pieces, -0.22, 0.18) * result
    return jnp.clip(result, min=-limit, max=limit).astype(held_as)


def setup_inputs(seed: int = 0, part: int = 0) -> dict:
    key_of = jax.random.split(jax.random.key(seed), 4)
    part_keys = jax.random.split(jax.random.fold_in(key_of[3], part), 4)
    raw_samples = bell_draw(part_keys[0], (2, INPUTS, SAMPLES), 1.0, 6.0, ((1, 16),), jnp.float32)
    prototype = bell_draw(key_of[1], (TAPS * FINE,), (TAPS * FINE) ** -0.5, 0.75, (), jnp.float32)
    beam_weight = bell_draw(part_keys[2], (2, NBEAM, INPUTS), (2 * INPUTS) ** -0.5, 0.09375, ((2, 16),))
    return {"raw_samples": raw_samples, "prototype": prototype, "beam_weight": beam_weight}


def filter_table(prototype):
    taps_fine = prototype.shape[0]
    sample = jnp.arange(taps_fine, dtype=jnp.int32) % FINE
    channel = jnp.arange(FINE, dtype=jnp.int32)
    phase_index = (sample[:, None] * channel[None, :]) % FINE
    phase_angle = phase_index.astype(jnp.float32) * (2.0 * math.pi / FINE)
    return prototype[:, None] * jnp.cos(phase_angle), -prototype[:, None] * jnp.sin(phase_angle)


def channelize(raw_samples, prototype):
    table_re, table_im = filter_table(prototype)
    inputs_here = raw_samples.shape[1]
    frames = DUMPS * MD
    shaped = raw_samples.reshape(2, inputs_here, frames + TAPS - 1, FINE)
    windows = jnp.concatenate([shaped[:, :, offset:offset + frames, :] for offset in range(TAPS)], axis=3)
    highest = lax.Precision.HIGHEST
    spec_re = jnp.einsum('bmn,nk->kbm', windows[0], table_re, precision=highest) - jnp.einsum('bmn,nk->kbm', windows[1], table_im, precision=highest)
    spec_im = jnp.einsum('bmn,nk->kbm', windows[0], table_im, precision=highest) + jnp.einsum('bmn,nk->kbm', windows[1], table_re, precision=highest)
    return spec_re, spec_im


def reference(raw_samples, prototype, beam_weight):
    spec_re, spec_im = channelize(raw_samples, prototype)
    spectra = jnp.stack([spec_re, spec_im]).astype(jnp.bfloat16)
    spectra = spectra.reshape(2, FINE, INPUTS, DUMPS, MD).transpose(0, 1, 3, 2, 4).reshape(2, FINE * DUMPS, INPUTS, MD)
    block_size = INPUTS // (STN_BLOCKS * CORE_BLOCKS)
    listed = spectra.reshape(2, FINE * DUMPS, STN_BLOCKS, CORE_BLOCKS, block_size, MD)
    listed = listed.transpose(0, 1, 3, 2, 4, 5).reshape(2, FINE * DUMPS, INPUTS, MD)

    def one_slot(slot_data):
        left_rows = jnp.concatenate([slot_data[0], slot_data[1]], axis=1)
        twisted = jnp.concatenate([-slot_data[1], slot_data[0]], axis=1)
        vis_re = jnp.dot(left_rows, left_rows.T, preferred_element_type=jnp.float32)
        vis_im = jnp.dot(left_rows, twisted.T, preferred_element_type=jnp.float32)
        return (jnp.stack([vis_re, vis_im]) * (1.0 / MD)).astype(jnp.bfloat16)

    visibility = lax.map(one_slot, listed.transpose(1, 0, 2, 3))
    real_rows = jnp.concatenate([beam_weight[0], -beam_weight[1]], axis=1)
    imag_rows = jnp.concatenate([beam_weight[1], beam_weight[0]], axis=1)

    def beam_slot(slot_data):
        stacked = jnp.concatenate([slot_data[0], slot_data[1]], axis=0)
        beam_re = jnp.dot(real_rows, stacked, preferred_element_type=jnp.float32)
        beam_im = jnp.dot(imag_rows, stacked, preferred_element_type=jnp.float32)
        return jnp.stack([beam_re, beam_im])

    beam_out = lax.map(beam_slot, spectra.transpose(1, 0, 2, 3)).transpose(1, 0, 2, 3)
    return visibility, beam_out
```

```python
import functools
import math

import jax
import jax.numpy as jnp
from jax import lax
from jax.experimental import pallas as pl
from jax.experimental.pallas import tpu as pltpu
from jax.sharding import PartitionSpec as P

FINE = 16
TAPS = 4
NBEAM = 512
DUMPS = 2
MD = 256


def filter_table(prototype):
    taps_fine = prototype.shape[0]
    sample = jnp.arange(taps_fine, dtype=jnp.int32) % FINE
    channel = jnp.arange(FINE, dtype=jnp.int32)
    phase_index = sample[:, None] * channel[None, :] % FINE
    phase_angle = phase_index.astype(jnp.float32) * (2.0 * math.pi / FINE)
    return (prototype[:, None] * jnp.cos(phase_angle), -prototype[:, None] * jnp.sin(phase_angle))


def channelize(raw_samples, prototype):
    table_re, table_im = filter_table(prototype)
    inputs_here = raw_samples.shape[1]
    frames = DUMPS * MD
    shaped = raw_samples.reshape(2, inputs_here, frames + TAPS - 1, FINE).transpose(0, 3, 1, 2)
    windows = jnp.concatenate(
        [shaped[:, :, :, offset : offset + frames] for offset in range(TAPS)], axis=1
    )
    highest = lax.Precision.HIGHEST
    spec_re = jnp.einsum("nk,nbm->kbm", table_re, windows[0], precision=highest) - jnp.einsum(
        "nk,nbm->kbm", table_im, windows[1], precision=highest
    )
    spec_im = jnp.einsum("nk,nbm->kbm", table_im, windows[0], precision=highest) + jnp.einsum(
        "nk,nbm->kbm", table_re, windows[1], precision=highest
    )
    spectra = jnp.stack([spec_re, spec_im]).astype(jnp.bfloat16)
    spectra = spectra.reshape(2, FINE, inputs_here, DUMPS, MD).transpose(0, 1, 3, 2, 4)
    return spectra.reshape(2, FINE * DUMPS, inputs_here, MD)


def form_beams(weights, rows_data):
    real_rows = jnp.concatenate([weights[0], -weights[1]], axis=1)
    imag_rows = jnp.concatenate([weights[1], weights[0]], axis=1)
    stacked = jnp.concatenate([rows_data[0], rows_data[1]], axis=1)
    beam_re = jnp.einsum("bn,snm->sbm", real_rows, stacked, preferred_element_type=jnp.float32)
    beam_im = jnp.einsum("bn,snm->sbm", imag_rows, stacked, preferred_element_type=jnp.float32)
    return jnp.stack([beam_re, beam_im])


def to_listed(weight_all, stations, cores, per_block):
    beams_here = weight_all.shape[1]
    weight_listed = weight_all.reshape(2, beams_here, stations, cores, per_block).transpose(
        0, 1, 3, 2, 4
    )
    return weight_listed.reshape(2, beams_here, stations * cores * per_block)


def per_device_plain(raw_samples, prototype, beam_weight):
    spectra = channelize(raw_samples, prototype)
    turned = lax.all_to_all(spectra, "stn", split_axis=1, concat_axis=2, tiled=True)
    col_left = jnp.concatenate([turned[0], turned[1]], axis=2)
    col_twist = jnp.concatenate([-turned[1], turned[0]], axis=2)
    beam_half = NBEAM // lax.axis_size("tile")
    stations = lax.axis_size("stn")
    cores = lax.axis_size("tile")
    per_block = beam_weight.shape[2]
    all_rows = lax.all_gather(turned, "tile", axis=2, tiled=True)
    row_left = jnp.concatenate([all_rows[0], all_rows[1]], axis=2)
    vis_re = jnp.einsum("snf,shf->snh", row_left, col_left, preferred_element_type=jnp.float32)
    vis_im = jnp.einsum("snf,shf->snh", row_left, col_twist, preferred_element_type=jnp.float32)
    visibility = (jnp.stack([vis_re, vis_im], axis=1) * (1.0 / MD)).astype(jnp.bfloat16)
    weight_all = lax.all_gather(beam_weight, ("stn", "tile"), axis=2, tiled=True)
    weight_listed = to_listed(weight_all, stations, cores, per_block)
    weight_mine = lax.dynamic_slice_in_dim(
        weight_listed, lax.axis_index("tile") * beam_half, beam_half, 1
    )
    beam_out = form_beams(weight_mine, all_rows)
    return (visibility, beam_out)


GROUP = 8
LANES = 128
STEP = 1024
SPAN = GROUP * FINE + (TAPS - 1) * FINE
TAIL = (TAPS - 1) * FINE


def window_table(prototype, channel):
    taps_fine = prototype.shape[0]
    sample = jnp.arange(taps_fine, dtype=jnp.int32) % FINE
    phase_index = channel[:, None] * sample[None, :] % FINE
    phase_angle = phase_index.astype(jnp.float32) * (2.0 * math.pi / FINE)
    re = prototype[None, :] * jnp.cos(phase_angle)
    im = -prototype[None, :] * jnp.sin(phase_angle)
    both = jnp.stack([jnp.stack([re, -im], axis=1), jnp.stack([im, re], axis=1)], axis=1)
    shifted = jnp.stack(
        [
            jnp.pad(both, ((0, 0), (0, 0), (0, 0), (FINE * f, SPAN - taps_fine - FINE * f)))
            for f in range(GROUP)
        ],
        axis=2,
    )
    table = shifted.reshape(channel.shape[0] * 2 * GROUP, 2 * SPAN)
    high = lax.reduce_precision(table, 8, 7)
    low = (table - high).astype(jnp.bfloat16)
    high = high.astype(jnp.bfloat16)
    return jnp.concatenate([high, low, high], axis=1)


def channelize_kernel(kh, table_ref, main_ref, next_ref, *refs):
    outs, window = refs[:-1], refs[-1]
    groups = STEP // (GROUP * FINE)
    for part in range(2):
        turned = jnp.concatenate([main_ref[part].T, next_ref[part].T[:TAIL]], axis=0)
        high = turned.astype(jnp.bfloat16)
        low = (turned - high.astype(jnp.float32)).astype(jnp.bfloat16)
        for j in range(groups):
            rows = slice(j * GROUP * FINE, j * GROUP * FINE + SPAN)
            cols = slice(j * LANES, (j + 1) * LANES)
            window[part * SPAN : (part + 1) * SPAN, cols] = high[rows]
            window[(2 + part) * SPAN : (3 + part) * SPAN, cols] = high[rows]
            window[(4 + part) * SPAN : (5 + part) * SPAN, cols] = low[rows]
    done = jnp.dot(table_ref[...], window[...], preferred_element_type=jnp.float32)
    for r, out in enumerate(outs):
        for kk in range(kh):
            for part in range(2):
                row = ((r * kh + kk) * 2 + part) * GROUP
                for j in range(0, groups, 2):
                    pair = jnp.concatenate(
                        [
                            done[row : row + GROUP, j * LANES : (j + 1) * LANES],
                            done[row : row + GROUP, (j + 1) * LANES : (j + 2) * LANES],
                        ],
                        axis=0,
                    )
                    out[kk, part, j * GROUP : (j + 2) * GROUP, :] = pair.astype(jnp.bfloat16)


def channelize_dump(raw_samples, table, dump, stations, kh):
    inputs_here = raw_samples.shape[1]
    steps = MD * FINE // STEP
    frames = STEP // FINE
    out = jax.ShapeDtypeStruct((kh, 2, MD, inputs_here), jnp.bfloat16)
    return pl.pallas_call(
        functools.partial(channelize_kernel, kh),
        grid=(steps,),
        in_specs=[
            pl.BlockSpec(table.shape, lambda i: (0, 0)),
            pl.BlockSpec((2, inputs_here, STEP), lambda i: (0, 0, dump * steps + i)),
            pl.BlockSpec(
                (2, inputs_here, LANES),
                lambda i: (0, 0, (dump * steps + i + 1) * (STEP // LANES)),
            ),
        ],
        out_specs=[pl.BlockSpec((kh, 2, frames, inputs_here), lambda i: (0, 0, i, 0))] * stations,
        out_shape=[out] * stations,
        scratch_shapes=[
            pltpu.VMEM((table.shape[1], STEP // (GROUP * FINE) * LANES), jnp.bfloat16)
        ],
        compiler_params=pltpu.CompilerParams(vmem_limit_bytes=40 << 20),
        cost_estimate=pl.CostEstimate(
            flops=2 * table.shape[0] * table.shape[1] * steps * 1024,
            bytes_accessed=inputs_here * MD * FINE * 12,
            transcendentals=0,
        ),
        name=f"channelize{dump}",
    )(table, raw_samples, raw_samples)


def place_kernel(count, where_ref, *refs):
    ins, out = refs[:count], refs[count]
    for r in range(count):
        at = pl.ds(pl.multiple_of(where_ref[r] * LANES, LANES), LANES)
        lead = ins[r].shape[:-2]
        for a in range(lead[0]):
            for b in range(lead[1]):
                rows = ins[r].shape[-2]
                out[a, b * rows : (b + 1) * rows, at] = ins[r][a, b]


def place(blocks, where, name):
    lead, two, rows, width = blocks[0].shape
    total = width * len(blocks)
    return pl.pallas_call(
        functools.partial(place_kernel, len(blocks)),
        grid_spec=pltpu.PrefetchScalarGridSpec(
            num_scalar_prefetch=1,
            grid=(lead,),
            in_specs=[pl.BlockSpec((1, two, rows, width), lambda i, w: (i, 0, 0, 0))] * len(blocks),
            out_specs=pl.BlockSpec((1, two * rows, total), lambda i, w: (i, 0, 0)),
        ),
        out_shape=jax.ShapeDtypeStruct((lead, two * rows, total), blocks[0].dtype),
        compiler_params=pltpu.CompilerParams(vmem_limit_bytes=30 << 20),
        cost_estimate=pl.CostEstimate(
            flops=0, bytes_accessed=4 * lead * two * rows * total, transcendentals=0
        ),
        name=name,
    )(where, *blocks)


def correlate_kernel(steps, rows, tile_ref, own_ref, other_ref, *refs):
    out_ref, twist = refs[-2], refs[-1]
    step = pl.program_id(1)

    @pl.when(step == 0)
    def _():
        twist[:MD] = -own_ref[0, MD:]
        twist[MD:] = own_ref[0, :MD]

    def write(left_ref, at):
        left = left_ref[0, :, pl.ds(pl.multiple_of(at * rows, rows), rows)].T
        re = jnp.dot(left, own_ref[0], preferred_element_type=jnp.float32)
        out_ref[0, 0] = (re * (1.0 / MD)).astype(jnp.bfloat16)
        im = jnp.dot(left, twist[...], preferred_element_type=jnp.float32)
        out_ref[0, 1] = (im * (1.0 / MD)).astype(jnp.bfloat16)

    @pl.when(step < steps)
    def _():
        write(own_ref, step)

    @pl.when(step >= steps)
    def _():
        write(other_ref, step - steps)


def correlate(own, other, tile, slots, dump, before):
    kh, depth, width = own.shape
    rows = 512
    steps = width // rows
    spec = pl.BlockSpec((1, depth, width), lambda k, a, t: (k, 0, 0))
    operands = [tile, own, other] + ([] if before is None else [before])
    return pl.pallas_call(
        functools.partial(correlate_kernel, steps, rows),
        grid_spec=pltpu.PrefetchScalarGridSpec(
            num_scalar_prefetch=1,
            grid=(kh, 2 * steps),
            in_specs=[spec, spec] + ([] if before is None else [pl.BlockSpec(memory_space=pl.ANY)]),
            out_specs=pl.BlockSpec(
                (1, 2, rows, width),
                lambda k, a, t: (k * DUMPS + dump, 0, (a + t[0] * steps) % (2 * steps), 0),
            ),
            scratch_shapes=[pltpu.VMEM((depth, width), jnp.bfloat16)],
        ),
        out_shape=jax.ShapeDtypeStruct((slots, 2, 2 * width, width), jnp.bfloat16),
        input_output_aliases={} if before is None else {3: 0},
        compiler_params=pltpu.CompilerParams(vmem_limit_bytes=50 << 20),
        cost_estimate=pl.CostEstimate(
            flops=kh * 2 * 2 * 2 * width * width * depth,
            bytes_accessed=kh * 2 * 2 * 2 * width * width,
            transcendentals=0,
        ),
        name=f"correlate{dump}",
    )(*operands)


def beam_kernel(own_w, other_w, own_ref, other_ref, out_ref):
    dims = (((1,), (1,)), ((), ()))
    both = lax.dot_general(own_w[0], own_ref[0], dims, preferred_element_type=jnp.float32)
    both += lax.dot_general(other_w[0], other_ref[0], dims, preferred_element_type=jnp.float32)
    beams = own_w.shape[1] // 2
    out_ref[0, 0] = both[:beams, :MD] - both[beams:, MD:]
    out_ref[1, 0] = both[beams:, :MD] + both[:beams, MD:]


def beams_of(own_w, other_w, own, other, dump):
    kh, depth, width = own.shape
    rows = own_w.shape[1]
    fixed = pl.BlockSpec((1, rows, width), lambda k: (0, 0, 0))
    moving = pl.BlockSpec((1, depth, width), lambda k: (k, 0, 0))
    return pl.pallas_call(
        beam_kernel,
        grid=(kh,),
        in_specs=[fixed, pl.BlockSpec((1, rows, width), lambda k: (1, 0, 0)), moving, moving],
        out_specs=pl.BlockSpec((2, 1, rows // 2, MD), lambda k: (0, k, 0, 0)),
        out_shape=jax.ShapeDtypeStruct((2, kh, rows // 2, MD), jnp.float32),
        compiler_params=pltpu.CompilerParams(vmem_limit_bytes=40 << 20),
        cost_estimate=pl.CostEstimate(
            flops=kh * 4 * rows * width * depth,
            bytes_accessed=kh * 4 * width * depth + 4 * rows * width,
            transcendentals=0,
        ),
        name=f"beams{dump}",
    )(own_w, other_w, own, other)


def partners(count, mask):
    return [(a, a ^ mask) for a in range(count)]


def per_device_fast(raw_samples, prototype, beam_weight):
    stations = lax.axis_size("stn")
    me, tile = lax.axis_index("stn"), lax.axis_index("tile")
    slots = FINE * DUMPS // stations
    kh = slots // DUMPS
    where = me ^ jnp.arange(stations, dtype=jnp.int32)
    channel = (where[:, None] * kh + jnp.arange(kh, dtype=jnp.int32)[None, :]).reshape(-1)
    table = window_table(prototype, channel)
    beam_half = beam_weight.shape[1] // 2
    swap = [(0, 1), (1, 0)]

    parts = [channelize_dump(raw_samples, table, dump, stations, kh) for dump in range(DUMPS)]
    arrived = [
        [part[0]] + [lax.ppermute(part[r], "stn", partners(stations, r)) for r in range(1, stations)]
        for part in parts
    ]

    mine = lax.dynamic_slice_in_dim(beam_weight, tile * beam_half, beam_half, 1)
    theirs = lax.dynamic_slice_in_dim(beam_weight, (1 - tile) * beam_half, beam_half, 1)
    held = jnp.stack([mine, lax.ppermute(theirs, "tile", swap)])[None]
    mask = stations // 2
    while mask:
        other = lax.ppermute(held, "stn", partners(stations, mask))
        held = jnp.stack([held, other], axis=1).reshape(-1, *held.shape[1:])
        mask //= 2
    weights = place([held[r] for r in range(stations)], where, "weights")

    visibility, beams = None, []
    tile_index = tile.reshape(1).astype(jnp.int32)
    for dump in range(DUMPS):
        own = place(arrived[dump], where, f"place{dump}")
        other = lax.ppermute(own, "tile", swap)
        visibility = correlate(own, other, tile_index, slots, dump, visibility)
        beams.append(beams_of(weights, weights, own, other, dump))
    beam_out = jnp.stack(beams, axis=2).reshape(2, slots, beam_half, MD)
    return visibility, beam_out


def per_device(raw_samples, prototype, beam_weight):
    stations = lax.axis_size("stn")
    fits = (
        raw_samples.shape[1] == LANES
        and lax.axis_size("tile") == 2
        and stations & (stations - 1) == 0
        and FINE % stations == 0
    )
    if fits:
        return per_device_fast(raw_samples, prototype, beam_weight)
    return per_device_plain(raw_samples, prototype, beam_weight)


def solution(mesh):
    placed = (P(None, ("band", "stn", "tile"), None), P(), P(None, None, ("band", "stn", "tile")))
    return jax.shard_map(
        per_device,
        mesh=mesh,
        in_specs=placed,
        out_specs=(P(("band", "stn"), None, None, "tile"), P(None, ("band", "stn"), "tile", None)),
        check_vma=False,
    )
```

```python
import functools
import math

import jax
import jax.numpy as jnp
from jax import lax
from jax.experimental import pallas as pl
from jax.experimental.pallas import tpu as pltpu
from jax.sharding import PartitionSpec as P


FINE = 16
TAPS = 4
NBEAM = 512
DUMPS = 2
MD = 256


def filter_table(prototype):
    taps_fine = prototype.shape[0]
    sample = jnp.arange(taps_fine, dtype=jnp.int32) % FINE
    channel = jnp.arange(FINE, dtype=jnp.int32)
    phase_index = sample[:, None] * channel[None, :] % FINE
    phase_angle = phase_index.astype(jnp.float32) * (2.0 * math.pi / FINE)
    return (prototype[:, None] * jnp.cos(phase_angle), -prototype[:, None] * jnp.sin(phase_angle))


def channelize(raw_samples, prototype):
    table_re, table_im = filter_table(prototype)
    inputs_here = raw_samples.shape[1]
    frames = DUMPS * MD
    shaped = raw_samples.reshape(2, inputs_here, frames + TAPS - 1, FINE).transpose(0, 3, 1, 2)
    windows = jnp.concatenate(
        [shaped[:, :, :, offset : offset + frames] for offset in range(TAPS)], axis=1
    )
    highest = lax.Precision.HIGHEST
    spec_re = jnp.einsum("nk,nbm->kbm", table_re, windows[0], precision=highest) - jnp.einsum(
        "nk,nbm->kbm", table_im, windows[1], precision=highest
    )
    spec_im = jnp.einsum("nk,nbm->kbm", table_im, windows[0], precision=highest) + jnp.einsum(
        "nk,nbm->kbm", table_re, windows[1], precision=highest
    )
    spectra = jnp.stack([spec_re, spec_im]).astype(jnp.bfloat16)
    spectra = spectra.reshape(2, FINE, inputs_here, DUMPS, MD).transpose(0, 1, 3, 2, 4)
    return spectra.reshape(2, FINE * DUMPS, inputs_here, MD)


def form_beams(weights, rows_data):
    real_rows = jnp.concatenate([weights[0], -weights[1]], axis=1)
    imag_rows = jnp.concatenate([weights[1], weights[0]], axis=1)
    stacked = jnp.concatenate([rows_data[0], rows_data[1]], axis=1)
    beam_re = jnp.einsum("bn,snm->sbm", real_rows, stacked, preferred_element_type=jnp.float32)
    beam_im = jnp.einsum("bn,snm->sbm", imag_rows, stacked, preferred_element_type=jnp.float32)
    return jnp.stack([beam_re, beam_im])


def to_listed(weight_all, stations, cores, per_block):
    beams_here = weight_all.shape[1]
    weight_listed = weight_all.reshape(2, beams_here, stations, cores, per_block).transpose(
        0, 1, 3, 2, 4
    )
    return weight_listed.reshape(2, beams_here, stations * cores * per_block)


def per_device_plain(raw_samples, prototype, beam_weight):
    spectra = channelize(raw_samples, prototype)
    turned = lax.all_to_all(spectra, "stn", split_axis=1, concat_axis=2, tiled=True)
    col_left = jnp.concatenate([turned[0], turned[1]], axis=2)
    col_twist = jnp.concatenate([-turned[1], turned[0]], axis=2)
    beam_half = NBEAM // lax.axis_size("tile")
    stations = lax.axis_size("stn")
    cores = lax.axis_size("tile")
    per_block = beam_weight.shape[2]
    all_rows = lax.all_gather(turned, "tile", axis=2, tiled=True)
    row_left = jnp.concatenate([all_rows[0], all_rows[1]], axis=2)
    vis_re = jnp.einsum("snf,shf->snh", row_left, col_left, preferred_element_type=jnp.float32)
    vis_im = jnp.einsum("snf,shf->snh", row_left, col_twist, preferred_element_type=jnp.float32)
    visibility = (jnp.stack([vis_re, vis_im], axis=1) * (1.0 / MD)).astype(jnp.bfloat16)
    weight_all = lax.all_gather(beam_weight, ("stn", "tile"), axis=2, tiled=True)
    weight_listed = to_listed(weight_all, stations, cores, per_block)
    weight_mine = lax.dynamic_slice_in_dim(
        weight_listed, lax.axis_index("tile") * beam_half, beam_half, 1
    )
    beam_out = form_beams(weight_mine, all_rows)
    return (visibility, beam_out)


GROUP = 8
LANES = 128
STEP = 1024
SPAN = GROUP * FINE + (TAPS - 1) * FINE
TAIL = (TAPS - 1) * FINE


def window_table(prototype, channel):
    taps_fine = prototype.shape[0]
    sample = jnp.arange(taps_fine, dtype=jnp.int32) % FINE
    phase_index = channel[:, None] * sample[None, :] % FINE
    phase_angle = phase_index.astype(jnp.float32) * (2.0 * math.pi / FINE)
    re = prototype[None, :] * jnp.cos(phase_angle)
    im = -prototype[None, :] * jnp.sin(phase_angle)
    both = jnp.stack([jnp.stack([re, -im], axis=1), jnp.stack([im, re], axis=1)], axis=1)
    shifted = jnp.stack(
        [
            jnp.pad(both, ((0, 0), (0, 0), (0, 0), (FINE * f, SPAN - taps_fine - FINE * f)))
            for f in range(GROUP)
        ],
        axis=2,
    )
    table = shifted.reshape(channel.shape[0] * 2 * GROUP, 2 * SPAN)
    high = lax.reduce_precision(table, 8, 7)
    low = (table - high).astype(jnp.bfloat16)
    high = high.astype(jnp.bfloat16)
    return jnp.concatenate([high, low, high], axis=1)


def channelize_kernel(tokens, table_ref, main_ref, next_ref, *refs):
    outs, window = refs[tokens:-1], refs[-1]
    groups = STEP // (GROUP * FINE)
    for part in range(2):
        samples = jnp.concatenate([main_ref[part], next_ref[part, :TAIL]], axis=0)
        high = samples.astype(jnp.bfloat16)
        low = (samples - high.astype(jnp.float32)).astype(jnp.bfloat16)
        for j in range(groups):
            rows = slice(j * GROUP * FINE, j * GROUP * FINE + SPAN)
            cols = slice(j * LANES, (j + 1) * LANES)
            window[part * SPAN : (part + 1) * SPAN, cols] = high[rows]
            window[(2 + part) * SPAN : (3 + part) * SPAN, cols] = high[rows]
            window[(4 + part) * SPAN : (5 + part) * SPAN, cols] = low[rows]
    done = jnp.dot(table_ref[...], window[...], preferred_element_type=jnp.float32)
    lead = outs[0].shape[0]
    for n in range(len(outs) * lead):
        for part in range(2):
            row = (n * 2 + part) * GROUP
            for j in range(0, groups, 2):
                pair = jnp.concatenate(
                    [
                        done[row : row + GROUP, j * LANES : (j + 1) * LANES],
                        done[row : row + GROUP, (j + 1) * LANES : (j + 2) * LANES],
                    ],
                    axis=0,
                )
                at = slice(j * GROUP, (j + 2) * GROUP)
                outs[n // lead][n % lead, part, at, :] = pair.astype(jnp.bfloat16)


def channelize_dump(turned, table, dump, count, lead, after):
    inputs_here = turned.shape[2]
    steps = MD * FINE // STEP
    frames = STEP // FINE
    ahead = 64
    out = jax.ShapeDtypeStruct((lead, 2, MD, inputs_here), jnp.bfloat16)
    return pl.pallas_call(
        functools.partial(channelize_kernel, len(after)),
        grid=(steps,),
        in_specs=[
            pl.BlockSpec(table.shape, lambda i: (0, 0)),
            pl.BlockSpec((2, STEP, inputs_here), lambda i: (0, dump * steps + i, 0)),
            pl.BlockSpec(
                (2, ahead, inputs_here),
                lambda i: (0, (dump * steps + i + 1) * (STEP // ahead), 0),
            ),
        ]
        + [pl.BlockSpec(memory_space=pl.ANY)] * len(after),
        out_specs=[pl.BlockSpec((lead, 2, frames, inputs_here), lambda i: (0, 0, i, 0))] * count,
        out_shape=[out] * count,
        scratch_shapes=[
            pltpu.VMEM((table.shape[1], STEP // (GROUP * FINE) * LANES), jnp.bfloat16)
        ],
        compiler_params=pltpu.CompilerParams(vmem_limit_bytes=58 << 20),
        cost_estimate=pl.CostEstimate(
            flops=2 * table.shape[0] * table.shape[1] * steps * 1024,
            bytes_accessed=inputs_here * MD * FINE * 12,
            transcendentals=0,
        ),
    )(table, turned, turned, *after)


def place_kernel(count, where_ref, *refs):
    ins, out = refs[:count], refs[-1]
    r = 0
    for ref in ins:
        pieces, _, two, rows, _ = ref.shape
        for n in range(pieces):
            at = pl.ds(pl.multiple_of(where_ref[r] * LANES, LANES), LANES)
            for b in range(two):
                out[0, b * rows : (b + 1) * rows, at] = ref[n, 0, b]
            r += 1


def place(blocks, where, after):
    lead, two, rows, width = blocks[0].shape[1:]
    total = width * sum(block.shape[0] for block in blocks)
    return pl.pallas_call(
        functools.partial(place_kernel, len(blocks)),
        grid_spec=pltpu.PrefetchScalarGridSpec(
            num_scalar_prefetch=1,
            grid=(lead,),
            in_specs=[
                pl.BlockSpec((block.shape[0], 1, two, rows, width), lambda i, w: (0, i, 0, 0, 0))
                for block in blocks
            ]
            + [pl.BlockSpec(memory_space=pl.ANY)] * len(after),
            out_specs=pl.BlockSpec((1, two * rows, total), lambda i, w: (i, 0, 0)),
        ),
        out_shape=jax.ShapeDtypeStruct((lead, two * rows, total), blocks[0].dtype),
        compiler_params=pltpu.CompilerParams(vmem_limit_bytes=30 << 20),
        cost_estimate=pl.CostEstimate(
            flops=0, bytes_accessed=4 * lead * two * rows * total, transcendentals=0
        ),
    )(where, *blocks, *after)


def correlate_kernel(rows, tile_ref, left_ref, right_ref, *refs):
    out_ref, twist = refs[-2], refs[-1]
    step = pl.program_id(1)

    @pl.when(step == 0)
    def _():
        twist[:MD] = -right_ref[0, MD:]
        twist[MD:] = right_ref[0, :MD]

    left = left_ref[0, :, pl.ds(pl.multiple_of(step * rows, rows), rows)].T
    re = jnp.dot(left, right_ref[0], preferred_element_type=jnp.float32)
    out_ref[0, 0] = (re * (1.0 / MD)).astype(jnp.bfloat16)
    im = jnp.dot(left, twist[...], preferred_element_type=jnp.float32)
    out_ref[0, 1] = (im * (1.0 / MD)).astype(jnp.bfloat16)


def correlate(left, right, half, slots, first, before):
    kh, depth, width = right.shape
    rows = 512
    steps = width // rows
    spec = pl.BlockSpec((1, depth, width), lambda k, a, t: (k, 0, 0))
    held = [] if before is None else [before]
    return pl.pallas_call(
        functools.partial(correlate_kernel, rows),
        grid_spec=pltpu.PrefetchScalarGridSpec(
            num_scalar_prefetch=1,
            grid=(kh, steps),
            in_specs=[spec, spec] + [pl.BlockSpec(memory_space=pl.ANY)] * len(held),
            out_specs=pl.BlockSpec(
                (1, 2, rows, width),
                lambda k, a, t: (k * DUMPS + first, 0, a + t[0] * steps, 0),
            ),
            scratch_shapes=[pltpu.VMEM((depth, width), jnp.bfloat16)],
        ),
        out_shape=jax.ShapeDtypeStruct((slots, 2, 2 * width, width), jnp.bfloat16),
        input_output_aliases={3: 0} if held else {},
        compiler_params=pltpu.CompilerParams(vmem_limit_bytes=40 << 20),
        cost_estimate=pl.CostEstimate(
            flops=kh * 2 * 2 * width * width * depth,
            bytes_accessed=kh * 2 * 2 * width * width,
            transcendentals=0,
        ),
    )(half, left, right, *held)


def beam_kernel(own_w, other_w, own_ref, other_ref, *refs):
    out_ref = refs[-1]
    dims = (((1,), (1,)), ((), ()))
    both = lax.dot_general(own_w[0], own_ref[0], dims, preferred_element_type=jnp.float32)
    both += lax.dot_general(other_w[0], other_ref[0], dims, preferred_element_type=jnp.float32)
    beams = own_w.shape[1] // 2
    out_ref[0, 0] = both[:beams, :MD] - both[beams:, MD:]
    out_ref[1, 0] = both[beams:, :MD] + both[:beams, MD:]


def beams_of(weights, own, other, slots, first, before):
    kh, depth, width = own.shape
    rows = weights.shape[1]
    held = [] if before is None else [before]
    moving = pl.BlockSpec((1, depth, width), lambda k: (k, 0, 0))
    return pl.pallas_call(
        beam_kernel,
        grid=(kh,),
        in_specs=[
            pl.BlockSpec((1, rows, width), lambda k: (0, 0, 0)),
            pl.BlockSpec((1, rows, width), lambda k: (1, 0, 0)),
            moving,
            moving,
        ]
        + [pl.BlockSpec(memory_space=pl.ANY)] * len(held),
        out_specs=pl.BlockSpec((2, 1, rows // 2, MD), lambda k: (0, k * DUMPS + first, 0, 0)),
        out_shape=jax.ShapeDtypeStruct((2, slots, rows // 2, MD), jnp.float32),
        input_output_aliases={4: 0} if held else {},
        compiler_params=pltpu.CompilerParams(vmem_limit_bytes=40 << 20),
        cost_estimate=pl.CostEstimate(
            flops=kh * 4 * rows * width * depth,
            bytes_accessed=kh * 4 * width * depth + 4 * rows * width,
            transcendentals=0,
        ),
    )(weights, weights, own, other, *held)


def partners(count, mask):
    return [(a, a ^ mask) for a in range(count)]


def per_device_fast(raw_samples, prototype, beam_weight):
    stations = lax.axis_size("stn")
    me, tile = lax.axis_index("stn"), lax.axis_index("tile")
    slots = FINE * DUMPS // stations
    kh = slots // DUMPS
    where = me ^ jnp.arange(stations, dtype=jnp.int32)
    channel = (where[:, None] * kh + jnp.arange(kh, dtype=jnp.int32)[None, :]).reshape(-1)
    table = window_table(prototype, channel)
    beam_half = beam_weight.shape[1] // 2
    swap = [(0, 1), (1, 0)]

    mine = lax.dynamic_slice_in_dim(beam_weight, tile * beam_half, beam_half, 1)
    theirs = lax.dynamic_slice_in_dim(beam_weight, (1 - tile) * beam_half, beam_half, 1)
    held = [jnp.stack([mine, lax.ppermute(theirs, "tile", swap)])[None]]
    order, stages, mask = [0], [], stations // 2
    while mask:
        whole = jnp.concatenate(held) if len(held) > 1 else held[0]
        held = [whole, lax.ppermute(whole, "stn", partners(stations, mask))]
        order = order + [o ^ mask for o in order]
        stages.append(held[1])
        mask //= 2

    turned = raw_samples.transpose(0, 2, 1)
    parts = []
    for dump in range(DUMPS):
        after = [parts[-1][0], stages[0]] if parts else []
        lead = 1 if dump else kh
        count = stations * kh // lead
        parts.append(channelize_dump(turned, table, dump, count, lead, after))

    chunks = [(0, list(range(kh)))] + [(d, [k]) for d in range(1, DUMPS) for k in range(kh)]
    arrived = []
    for dump, ks in chunks:
        blocks = [None] * stations
        for r in reversed(range(stations)):
            sent = parts[dump][r if dump == 0 else r * kh + ks[0]][None]
            blocks[r] = lax.ppermute(sent, "stn", partners(stations, r)) if r else sent
        arrived.append(blocks)

    visibility, beam_out, weights, after = None, None, None, [stages[1 % len(stages)], parts[-1][0]]
    own_half = tile.reshape(1).astype(jnp.int32)
    for n, (dump, ks) in enumerate(chunks):
        first = ks[0] * DUMPS + dump
        own = place(arrived[n], where, after)
        other = lax.ppermute(own, "tile", swap)
        visibility = correlate(own, own, own_half, slots, first, visibility)
        visibility = correlate(other, own, 1 - own_half, slots, first, visibility)
        if weights is None:
            spots = me ^ jnp.asarray(order, dtype=jnp.int32)
            weights = place(held, spots, [])
        beam_out = beams_of(weights, own, other, slots, first, beam_out)
        after = [visibility, beam_out] if n else [visibility]
    return visibility, beam_out


def per_device(raw_samples, prototype, beam_weight):
    stations = lax.axis_size("stn")
    fits = (
        raw_samples.shape[1] == LANES
        and lax.axis_size("tile") == 2
        and stations & (stations - 1) == 0
        and FINE % stations == 0
    )
    if fits:
        return per_device_fast(raw_samples, prototype, beam_weight)
    return per_device_plain(raw_samples, prototype, beam_weight)


def solution(mesh):
    placed = (P(None, ("band", "stn", "tile"), None), P(), P(None, None, ("band", "stn", "tile")))
    return jax.shard_map(
        per_device,
        mesh=mesh,
        in_specs=placed,
        out_specs=(P(("band", "stn"), None, None, "tile"), P(None, ("band", "stn"), "tile", None)),
        check_vma=False,
    )
```

```python
import functools
import math

import jax
import jax.numpy as jnp
from jax import lax
from jax.experimental import pallas as pl
from jax.experimental.pallas import tpu as pltpu
from jax.sharding import PartitionSpec as P


FINE = 16
TAPS = 4
NBEAM = 512
DUMPS = 2
MD = 256


def filter_table(prototype):
    taps_fine = prototype.shape[0]
    sample = jnp.arange(taps_fine, dtype=jnp.int32) % FINE
    channel = jnp.arange(FINE, dtype=jnp.int32)
    phase_index = sample[:, None] * channel[None, :] % FINE
    phase_angle = phase_index.astype(jnp.float32) * (2.0 * math.pi / FINE)
    return (prototype[:, None] * jnp.cos(phase_angle), -prototype[:, None] * jnp.sin(phase_angle))


def channelize(raw_samples, prototype):
    table_re, table_im = filter_table(prototype)
    inputs_here = raw_samples.shape[1]
    frames = DUMPS * MD
    shaped = raw_samples.reshape(2, inputs_here, frames + TAPS - 1, FINE).transpose(0, 3, 1, 2)
    windows = jnp.concatenate(
        [shaped[:, :, :, offset : offset + frames] for offset in range(TAPS)], axis=1
    )
    highest = lax.Precision.HIGHEST
    spec_re = jnp.einsum("nk,nbm->kbm", table_re, windows[0], precision=highest) - jnp.einsum(
        "nk,nbm->kbm", table_im, windows[1], precision=highest
    )
    spec_im = jnp.einsum("nk,nbm->kbm", table_im, windows[0], precision=highest) + jnp.einsum(
        "nk,nbm->kbm", table_re, windows[1], precision=highest
    )
    spectra = jnp.stack([spec_re, spec_im]).astype(jnp.bfloat16)
    spectra = spectra.reshape(2, FINE, inputs_here, DUMPS, MD).transpose(0, 1, 3, 2, 4)
    return spectra.reshape(2, FINE * DUMPS, inputs_here, MD)


def form_beams(weights, rows_data):
    real_rows = jnp.concatenate([weights[0], -weights[1]], axis=1)
    imag_rows = jnp.concatenate([weights[1], weights[0]], axis=1)
    stacked = jnp.concatenate([rows_data[0], rows_data[1]], axis=1)
    beam_re = jnp.einsum("bn,snm->sbm", real_rows, stacked, preferred_element_type=jnp.float32)
    beam_im = jnp.einsum("bn,snm->sbm", imag_rows, stacked, preferred_element_type=jnp.float32)
    return jnp.stack([beam_re, beam_im])


def to_listed(weight_all, stations, cores, per_block):
    beams_here = weight_all.shape[1]
    weight_listed = weight_all.reshape(2, beams_here, stations, cores, per_block).transpose(
        0, 1, 3, 2, 4
    )
    return weight_listed.reshape(2, beams_here, stations * cores * per_block)


def per_device_plain(raw_samples, prototype, beam_weight):
    spectra = channelize(raw_samples, prototype)
    turned = lax.all_to_all(spectra, "stn", split_axis=1, concat_axis=2, tiled=True)
    col_left = jnp.concatenate([turned[0], turned[1]], axis=2)
    col_twist = jnp.concatenate([-turned[1], turned[0]], axis=2)
    beam_half = NBEAM // lax.axis_size("tile")
    stations = lax.axis_size("stn")
    cores = lax.axis_size("tile")
    per_block = beam_weight.shape[2]
    all_rows = lax.all_gather(turned, "tile", axis=2, tiled=True)
    row_left = jnp.concatenate([all_rows[0], all_rows[1]], axis=2)
    vis_re = jnp.einsum("snf,shf->snh", row_left, col_left, preferred_element_type=jnp.float32)
    vis_im = jnp.einsum("snf,shf->snh", row_left, col_twist, preferred_element_type=jnp.float32)
    visibility = (jnp.stack([vis_re, vis_im], axis=1) * (1.0 / MD)).astype(jnp.bfloat16)
    weight_all = lax.all_gather(beam_weight, ("stn", "tile"), axis=2, tiled=True)
    weight_listed = to_listed(weight_all, stations, cores, per_block)
    weight_mine = lax.dynamic_slice_in_dim(
        weight_listed, lax.axis_index("tile") * beam_half, beam_half, 1
    )
    beam_out = form_beams(weight_mine, all_rows)
    return (visibility, beam_out)


GROUP = 8
LANES = 128
STEP = 1024
SPAN = GROUP * FINE + (TAPS - 1) * FINE
TAIL = (TAPS - 1) * FINE


def window_table(prototype, channel):
    taps_fine = prototype.shape[0]
    sample = jnp.arange(taps_fine, dtype=jnp.int32) % FINE
    phase_index = channel[:, None] * sample[None, :] % FINE
    phase_angle = phase_index.astype(jnp.float32) * (2.0 * math.pi / FINE)
    re = prototype[None, :] * jnp.cos(phase_angle)
    im = -prototype[None, :] * jnp.sin(phase_angle)
    both = jnp.stack([jnp.stack([re, -im], axis=1), jnp.stack([im, re], axis=1)], axis=1)
    shifted = jnp.stack(
        [
            jnp.pad(both, ((0, 0), (0, 0), (0, 0), (FINE * f, SPAN - taps_fine - FINE * f)))
            for f in range(GROUP)
        ],
        axis=2,
    )
    table = shifted.reshape(channel.shape[0] * 2 * GROUP, 2 * SPAN)
    high = lax.reduce_precision(table, 8, 7)
    low = (table - high).astype(jnp.bfloat16)
    high = high.astype(jnp.bfloat16)
    return jnp.concatenate([high, low, high], axis=1)


def channelize_kernel(tokens, table_ref, main_ref, next_ref, *refs):
    outs, window = refs[tokens:-1], refs[-1]
    groups = STEP // (GROUP * FINE)
    for part in range(2):
        samples = jnp.concatenate([main_ref[part], next_ref[part, :TAIL]], axis=0)
        high = samples.astype(jnp.bfloat16)
        low = (samples - high.astype(jnp.float32)).astype(jnp.bfloat16)
        for j in range(groups):
            rows = slice(j * GROUP * FINE, j * GROUP * FINE + SPAN)
            cols = slice(j * LANES, (j + 1) * LANES)
            window[part * SPAN : (part + 1) * SPAN, cols] = high[rows]
            window[(2 + part) * SPAN : (3 + part) * SPAN, cols] = high[rows]
            window[(4 + part) * SPAN : (5 + part) * SPAN, cols] = low[rows]
    done = jnp.dot(table_ref[...], window[...], preferred_element_type=jnp.float32)
    lead = outs[0].shape[0]
    for n in range(len(outs) * lead):
        for part in range(2):
            row = (n * 2 + part) * GROUP
            for j in range(0, groups, 2):
                pair = jnp.concatenate(
                    [
                        done[row : row + GROUP, j * LANES : (j + 1) * LANES],
                        done[row : row + GROUP, (j + 1) * LANES : (j + 2) * LANES],
                    ],
                    axis=0,
                )
                at = slice(j * GROUP, (j + 2) * GROUP)
                outs[n // lead][n % lead, part, at, :] = pair.astype(jnp.bfloat16)


def channelize_dump(turned, table, dump, count, lead, after):
    inputs_here = turned.shape[2]
    steps = MD * FINE // STEP
    frames = STEP // FINE
    ahead = 64
    out = jax.ShapeDtypeStruct((lead, 2, MD, inputs_here), jnp.bfloat16)
    return pl.pallas_call(
        functools.partial(channelize_kernel, len(after)),
        grid=(steps,),
        in_specs=[
            pl.BlockSpec(table.shape, lambda i: (0, 0)),
            pl.BlockSpec((2, STEP, inputs_here), lambda i: (0, dump * steps + i, 0)),
            pl.BlockSpec(
                (2, ahead, inputs_here),
                lambda i: (0, (dump * steps + i + 1) * (STEP // ahead), 0),
            ),
        ]
        + [pl.BlockSpec(memory_space=pl.ANY)] * len(after),
        out_specs=[pl.BlockSpec((lead, 2, frames, inputs_here), lambda i: (0, 0, i, 0))] * count,
        out_shape=[out] * count,
        scratch_shapes=[
            pltpu.VMEM((table.shape[1], STEP // (GROUP * FINE) * LANES), jnp.bfloat16)
        ],
        compiler_params=pltpu.CompilerParams(vmem_limit_bytes=58 << 20),
        cost_estimate=pl.CostEstimate(
            flops=2 * table.shape[0] * table.shape[1] * steps * 1024,
            bytes_accessed=inputs_here * MD * FINE * 12,
            transcendentals=0,
        ),
    )(table, turned, turned, *after)


def place_kernel(count, where_ref, *refs):
    ins, out = refs[:count], refs[-1]
    r = 0
    for ref in ins:
        pieces, _, two, rows, _ = ref.shape
        for n in range(pieces):
            at = pl.ds(pl.multiple_of(where_ref[r] * LANES, LANES), LANES)
            for b in range(two):
                out[0, b * rows : (b + 1) * rows, at] = ref[n, 0, b]
            r += 1


def place(blocks, where, after):
    lead, two, rows, width = blocks[0].shape[1:]
    total = width * sum(block.shape[0] for block in blocks)
    return pl.pallas_call(
        functools.partial(place_kernel, len(blocks)),
        grid_spec=pltpu.PrefetchScalarGridSpec(
            num_scalar_prefetch=1,
            grid=(lead,),
            in_specs=[
                pl.BlockSpec((block.shape[0], 1, two, rows, width), lambda i, w: (0, i, 0, 0, 0))
                for block in blocks
            ]
            + [pl.BlockSpec(memory_space=pl.ANY)] * len(after),
            out_specs=pl.BlockSpec((1, two * rows, total), lambda i, w: (i, 0, 0)),
        ),
        out_shape=jax.ShapeDtypeStruct((lead, two * rows, total), blocks[0].dtype),
        compiler_params=pltpu.CompilerParams(vmem_limit_bytes=30 << 20),
        cost_estimate=pl.CostEstimate(
            flops=0, bytes_accessed=4 * lead * two * rows * total, transcendentals=0
        ),
    )(where, *blocks, *after)


def correlate_kernel(rows, tile_ref, left_ref, right_ref, *refs):
    out_ref, twist = refs[-2], refs[-1]
    step = pl.program_id(1)

    @pl.when(step == 0)
    def _():
        twist[:MD] = -right_ref[0, MD:]
        twist[MD:] = right_ref[0, :MD]

    left = left_ref[0, :, pl.ds(pl.multiple_of(step * rows, rows), rows)].T
    re = jnp.dot(left, right_ref[0], preferred_element_type=jnp.float32)
    out_ref[0, 0] = (re * (1.0 / MD)).astype(jnp.bfloat16)
    im = jnp.dot(left, twist[...], preferred_element_type=jnp.float32)
    out_ref[0, 1] = (im * (1.0 / MD)).astype(jnp.bfloat16)


def correlate(left, right, half, slots, first, before):
    kh, depth, width = right.shape
    rows = 512
    steps = width // rows
    spec = pl.BlockSpec((1, depth, width), lambda k, a, t: (k, 0, 0))
    held = [] if before is None else [before]
    return pl.pallas_call(
        functools.partial(correlate_kernel, rows),
        grid_spec=pltpu.PrefetchScalarGridSpec(
            num_scalar_prefetch=1,
            grid=(kh, steps),
            in_specs=[spec, spec] + [pl.BlockSpec(memory_space=pl.ANY)] * len(held),
            out_specs=pl.BlockSpec(
                (1, 2, rows, width),
                lambda k, a, t: (k * DUMPS + first, 0, a + t[0] * steps, 0),
            ),
            scratch_shapes=[pltpu.VMEM((depth, width), jnp.bfloat16)],
        ),
        out_shape=jax.ShapeDtypeStruct((slots, 2, 2 * width, width), jnp.bfloat16),
        input_output_aliases={3: 0} if held else {},
        compiler_params=pltpu.CompilerParams(vmem_limit_bytes=40 << 20),
        cost_estimate=pl.CostEstimate(
            flops=kh * 2 * 2 * width * width * depth,
            bytes_accessed=kh * 2 * 2 * width * width,
            transcendentals=0,
        ),
    )(half, left, right, *held)


def beam_kernel(own_w, other_w, own_ref, other_ref, *refs):
    out_ref = refs[-1]
    dims = (((1,), (1,)), ((), ()))
    both = lax.dot_general(own_w[0], own_ref[0], dims, preferred_element_type=jnp.float32)
    both += lax.dot_general(other_w[0], other_ref[0], dims, preferred_element_type=jnp.float32)
    beams = own_w.shape[1] // 2
    out_ref[0, 0] = both[:beams, :MD] - both[beams:, MD:]
    out_ref[1, 0] = both[beams:, :MD] + both[:beams, MD:]


def beams_of(weights, own, other, slots, first, before):
    kh, depth, width = own.shape
    rows = weights.shape[1]
    held = [] if before is None else [before]
    moving = pl.BlockSpec((1, depth, width), lambda k: (k, 0, 0))
    return pl.pallas_call(
        beam_kernel,
        grid=(kh,),
        in_specs=[
            pl.BlockSpec((1, rows, width), lambda k: (0, 0, 0)),
            pl.BlockSpec((1, rows, width), lambda k: (1, 0, 0)),
            moving,
            moving,
        ]
        + [pl.BlockSpec(memory_space=pl.ANY)] * len(held),
        out_specs=pl.BlockSpec((2, 1, rows // 2, MD), lambda k: (0, k * DUMPS + first, 0, 0)),
        out_shape=jax.ShapeDtypeStruct((2, slots, rows // 2, MD), jnp.float32),
        input_output_aliases={4: 0} if held else {},
        compiler_params=pltpu.CompilerParams(vmem_limit_bytes=40 << 20),
        cost_estimate=pl.CostEstimate(
            flops=kh * 4 * rows * width * depth,
            bytes_accessed=kh * 4 * width * depth + 4 * rows * width,
            transcendentals=0,
        ),
    )(weights, weights, own, other, *held)


def partners(count, mask):
    return [(a, a ^ mask) for a in range(count)]


def per_device_fast(raw_samples, prototype, beam_weight):
    stations = lax.axis_size("stn")
    me, tile = lax.axis_index("stn"), lax.axis_index("tile")
    slots = FINE * DUMPS // stations
    kh = slots // DUMPS
    where = me ^ jnp.arange(stations, dtype=jnp.int32)
    channel = (where[:, None] * kh + jnp.arange(kh, dtype=jnp.int32)[None, :]).reshape(-1)
    table = window_table(prototype, channel)
    beam_half = beam_weight.shape[1] // 2
    swap = [(0, 1), (1, 0)]

    mine = lax.dynamic_slice_in_dim(beam_weight, tile * beam_half, beam_half, 1)
    theirs = lax.dynamic_slice_in_dim(beam_weight, (1 - tile) * beam_half, beam_half, 1)
    held = [jnp.stack([mine, lax.ppermute(theirs, "tile", swap)])[None]]
    order, stages, mask = [0], [], stations // 2
    while mask:
        whole = jnp.concatenate(held) if len(held) > 1 else held[0]
        held = [whole, lax.ppermute(whole, "stn", partners(stations, mask))]
        order = order + [o ^ mask for o in order]
        stages.append(held[1])
        mask //= 2

    turned = raw_samples.transpose(0, 2, 1)
    parts = []
    for dump in range(DUMPS):
        after = [parts[-1][0], stages[0]] if parts else []
        parts.append(channelize_dump(turned, table, dump, stations * kh, 1, after))

    chunks = [(dump, k) for dump in range(DUMPS) for k in range(kh)]
    arrived = []
    for dump, k in chunks:
        blocks = [None] * stations
        for r in reversed(range(stations)):
            sent = parts[dump][r * kh + k][None]
            blocks[r] = lax.ppermute(sent, "stn", partners(stations, r)) if r else sent
        arrived.append(blocks)

    visibility, beam_out, weights, after = None, None, None, [stages[1 % len(stages)], parts[-1][0]]
    own_half = tile.reshape(1).astype(jnp.int32)
    for n, (dump, k) in enumerate(chunks):
        first = k * DUMPS + dump
        own = place(arrived[n], where, after)
        other = lax.ppermute(own, "tile", swap)
        visibility = correlate(own, own, own_half, slots, first, visibility)
        visibility = correlate(other, own, 1 - own_half, slots, first, visibility)
        if weights is None:
            spots = me ^ jnp.asarray(order, dtype=jnp.int32)
            weights = place(held, spots, [])
        beam_out = beams_of(weights, own, other, slots, first, beam_out)
        after = [visibility]
    return visibility, beam_out


def per_device(raw_samples, prototype, beam_weight):
    stations = lax.axis_size("stn")
    fits = (
        raw_samples.shape[1] == LANES
        and lax.axis_size("tile") == 2
        and stations & (stations - 1) == 0
        and FINE % stations == 0
    )
    if fits:
        return per_device_fast(raw_samples, prototype, beam_weight)
    return per_device_plain(raw_samples, prototype, beam_weight)


def solution(mesh):
    placed = (P(None, ("band", "stn", "tile"), None), P(), P(None, None, ("band", "stn", "tile")))
    return jax.shard_map(
        per_device,
        mesh=mesh,
        in_specs=placed,
        out_specs=(P(("band", "stn"), None, None, "tile"), P(None, ("band", "stn"), "tile", None)),
        check_vma=False,
    )
```
